512 devices in a mesh: layer: 16 (over z_lo, x), tok: 32 (over z_hi, y, core).
Axes of the slice: x: 4, y: 4, z: 16 (z_hi: 4, z_lo: 4; z = z_hi * 4 + z_lo), core: 2. Of those that a mesh axis runs over, the one named last changes fastest.
Arguments:
- inputs: bfloat16 [16, 8192, 2048], P('layer', 'tok'), may hold values from -6 to 6
- enc_weight: bfloat16 [4, 2048, 1024], P(None, 'tok'), may hold values from -0.125 to 0.125
- enc_bias: float32 [4, 1024], replicated, may hold values from -0.5 to 0.5
- dec_weight: bfloat16 [10, 1024, 2048], P(None, 'tok'), may hold values from -0.1875 to 0.1875
- dec_bias: float32 [4, 2048], replicated, may hold values from -3 to 3
Outputs:
- rebuilt: bfloat16 [16, 4, 8192, 512], P('layer', None, 'tok')
The draws below stay inside these ranges and needn't reach their ends.
All inputs are finite; a program needn't handle non-finite values.
Results may differ from the reference program's by a relative error of at most 0.0046.
Values may be sent and summed in bfloat16 or wider, within the bound.
No kernel may reach another device: no remote copies, remote signals or barrier semaphores. Data moves between devices by JAX's collectives and lax.ppermute only.
A program may use at most 64 MiB of HBM per device.

```python
import jax
import jax.numpy as jnp

D = 2048
F = 1024
LAYERS = 4
COLS = 4
ROWS = 8192
PAIRS = 10
N_LAYER = 16


def levels(own_key, shape, split, least, top_value):
    loudness, own = 1.0, jax.random.fold_in(own_key, 6)
    for position, blocks in split:
        draws = jnp.exp(jax.random.uniform(jax.random.fold_in(own, position), (blocks,), jnp.float32, least / len(split), top_value / len(split)))
        loudness = loudness * jnp.repeat(draws, shape[position] // blocks).reshape([-1 if axis == position else 1 for axis in range(len(shape))])
    return loudness


def centred(key, shape, spread, reach, pieces=(), held_as=jnp.bfloat16):
    array = jax.random.normal(key, shape, jnp.float32) * spread
    if len(pieces) > 0:
        array = levels(key, shape, pieces, -0.22, 0.18) * array
    return jnp.clip(array, min=-reach, max=reach).astype(held_as)


def setup_inputs(seed: int = 0) -> dict:
    streams_of = jax.random.split(jax.random.key(seed), 6)
    return {
        "inputs": centred(streams_of[0], (N_LAYER, ROWS, D), 1.0, 6.0, ((0, 16), (1, 32))),
        "enc_weight": centred(streams_of[1], (LAYERS, D, F), D ** -0.5, 0.125, ((1, 32),)),
        "enc_bias": jnp.clip(jax.random.uniform(streams_of[2], (LAYERS, F), jnp.float32, -0.5, 0.5), -0.5, 0.5),
        "dec_weight": centred(streams_of[3], (PAIRS, F, D), F ** -0.5, 0.1875, ((1, 32),)),
        "dec_bias": centred(streams_of[4], (LAYERS, D), 0.5, 3.0, (), jnp.float32),
    }


def reference(inputs, enc_weight, enc_bias, dec_weight, dec_bias):
    stacked = inputs.reshape(LAYERS, COLS * ROWS, D)
    latent_list = []
    for layer_index in range(LAYERS):
        preact = jnp.dot(stacked[layer_index], enc_weight[layer_index], preferred_element_type=jnp.float32)
        latent_list.append(jnp.maximum(preact + enc_bias[layer_index].astype(jnp.float32), 0.0).astype(jnp.bfloat16))
    outputs = []
    for target in range(LAYERS):
        summed = jnp.zeros((COLS * ROWS, D), jnp.float32)
        for source in range(target + 1):
            summed = summed + jnp.dot(latent_list[source], dec_weight[target * (target + 1) // 2 + source], preferred_element_type=jnp.float32)
        rebuilt = (summed + dec_bias[target].astype(jnp.float32)).astype(jnp.bfloat16)
        rebuilt = rebuilt.reshape(COLS, ROWS, COLS, D // COLS).transpose(2, 0, 1, 3)
        outputs.append(rebuilt)
    return jnp.stack(outputs).reshape(N_LAYER, COLS, ROWS, D // COLS)
```

```python
import jax
import jax.numpy as jnp
from jax import lax
from jax.sharding import Mesh, PartitionSpec as P

AXES = ("zl", "x", "zh", "y", "core")
LAYER = ("zl", "x")
TOK = ("zh", "y", "core")


def ring(size, step):
    return [(i, (i + step) % size) for i in range(size)]


def spread(block, axis):
    size = lax.axis_size(axis)
    return lax.all_to_all(
        jnp.broadcast_to(block[None], (size, *block.shape)), axis, 0, 0, tiled=True
    )


def body(inputs, enc_weight, enc_bias, dec_weight, dec_bias):
    layers, shard_rows, latent_count = enc_weight.shape
    width = dec_weight.shape[2]
    layer = lax.axis_index("zl")
    col = lax.axis_index("x")
    core = lax.axis_index("core")
    cols = lax.axis_size("x")
    zh_size, y_size = lax.axis_size("zh"), lax.axis_size("y")
    col_width = width // cols
    tokens = inputs.shape[1]
    half = latent_count // 2
    swap = [(0, 1), (1, 0)]

    blocks = []
    for slot in range(layers):
        pair = layer * (layer + 1) // 2 + jnp.maximum(layer - slot, 0)
        blocks.append(
            lax.dynamic_slice(
                dec_weight, (pair, 0, col * col_width), (1, dec_weight.shape[1], col_width)
            )
        )
    decoder = lax.all_gather(jnp.concatenate(blocks, 0), TOK, axis=1, tiled=True)

    own = lax.dynamic_index_in_dim(enc_weight, layer, 0, keepdims=False)
    mine = lax.dynamic_slice_in_dim(own, core * half, half, 1)
    other = lax.dynamic_slice_in_dim(own, (1 - core) * half, half, 1)
    arrived = lax.ppermute(other, "core", swap)
    first, second = jnp.where(core == 0, mine, arrived), jnp.where(core == 0, arrived, mine)
    pair_rows = jnp.concatenate([first, second], 0)
    part_rows = pair_rows.shape[0] // cols
    part = lax.dynamic_slice_in_dim(pair_rows, col * part_rows, part_rows, 0)
    over_z = spread(part, "zh")
    plane = spread(over_z, ("x", "y")).reshape(cols, y_size, zh_size, part_rows, half)
    encoder = plane.transpose(2, 1, 0, 3, 4).reshape(-1, half)

    token_rows = inputs[0]
    partner_rows = lax.ppermute(token_rows, "core", swap)
    bias = lax.dynamic_slice(enc_bias, (layer, core * half), (1, half))

    def encode(rows):
        preact = jnp.dot(rows, encoder, preferred_element_type=jnp.float32)
        return jnp.maximum(preact + bias, 0.0).astype(jnp.bfloat16)

    both = encode(jnp.concatenate([token_rows, partner_rows], 0))
    here, there = both[:tokens], both[tokens:]
    back = lax.ppermute(there, "core", swap)
    latents = jnp.where(
        core == 0,
        jnp.concatenate([here, back], 1),
        jnp.concatenate([back, here], 1),
    )

    total = None
    held = latents
    for slot in range(layers):
        following = None
        if slot < layers - 1:
            following = lax.ppermute(held, "zl", [(i, i + 1) for i in range(slot, layers - 1)])
        from_left = lax.ppermute(held, "x", ring(cols, 1))
        from_right = lax.ppermute(held, "x", ring(cols, -1))
        mid = tokens // 2
        far_top = lax.ppermute(from_left[:mid], "x", ring(cols, 1))
        far_bottom = lax.ppermute(from_right[mid:], "x", ring(cols, -1))
        stacked = jnp.concatenate([held, from_right, far_top, far_bottom, from_left], 0)
        product = jnp.dot(stacked, decoder[slot], preferred_element_type=jnp.float32)
        total = product if total is None else total + product
        held = following
    group_bias = lax.dynamic_slice(dec_bias, (layer, col * col_width), (1, col_width))
    rebuilt = (total + group_bias).astype(jnp.bfloat16).reshape(cols, tokens, col_width)
    twice = jnp.concatenate([rebuilt, rebuilt], 0)
    return lax.dynamic_slice_in_dim(twice, (cols - col) % cols, cols, 0)[None]


def solution(mesh):
    names = dict(zip(mesh.axis_names, mesh.devices.shape))
    layers = 4
    cols = names["layer"] // layers
    cores = 2
    zh_size = 4
    y_size = names["tok"] // (zh_size * cores)
    grid = Mesh(mesh.devices.reshape(layers, cols, zh_size, y_size, cores), AXES)
    in_specs = (P(LAYER, TOK, None), P(None, TOK, None), P(), P(None, TOK, None), P())
    out_specs = P(LAYER, None, TOK, None)
    return jax.shard_map(body, mesh=grid, in_specs=in_specs, out_specs=out_specs, check_vma=False)
```

```python
import functools

import jax
import jax.numpy as jnp
from jax import lax
from jax.experimental import pallas as pl
from jax.experimental.pallas import tpu as pltpu
from jax.sharding import Mesh, PartitionSpec as P


AXES = ("zl", "x", "zh", "y", "core")
LAYER = ("zl", "x")
TOK = ("zh", "y", "core")


def spread(block, axis):
    size = lax.axis_size(axis)
    return lax.all_to_all(
        jnp.broadcast_to(block[None], (size, *block.shape)), axis, 0, 0, tiled=True
    )


def exchange(block, flip, least):
    cols, layers = lax.axis_size("x"), lax.axis_size("zl")
    pairs = [
        (layer * cols + i, layer * cols + (cols - 1 - i if flip else i ^ 1))
        for layer in range(least, layers)
        for i in range(cols)
    ]
    return lax.ppermute(block, LAYER, pairs)


def halves(near, flipped, least):
    mid = near.shape[0] // 2
    top = exchange(near[:mid], True, least)
    bottom = exchange(flipped[mid:], False, least)
    return top, bottom


def at_step(col, cols, step):
    near = col + 1 - 2 * lax.rem(col, 2)
    return (col, near, cols - 1 - col, lax.rem(col + 2, cols))[step]


def encode_kernel(place, own, near, flip, top, bottom, mine, other, bias, out, weight):
    col, core = place[0], place[1]
    y_size, zh_size, rows, _ = mine.shape
    cols = out.shape[0] // own.shape[0]
    for zh in range(zh_size):
        for y in range(y_size):
            start = (zh * y_size + y) * 2 * rows
            weight[pl.ds(pl.multiple_of(start + core * rows, rows), rows), :] = mine[y, zh]
            weight[pl.ds(pl.multiple_of(start + (1 - core) * rows, rows), rows), :] = other[y, zh]
    tokens, mid = own.shape[0], top.shape[0]
    for step, part, offset in ((0, own, 0), (1, near, 0), (2, flip, 0), (3, top, 0), (3, bottom, mid)):
        group = at_step(col, cols, step)
        preact = jnp.dot(part[...], weight[...], preferred_element_type=jnp.float32)
        latents = jnp.maximum(preact + bias[...], 0.0).astype(out.dtype)
        out[pl.ds(pl.multiple_of(group * tokens + offset, mid), part.shape[0]), :] = latents


def encode(place, parts, mine, other, bias):
    tokens, depth = parts[0].shape
    cols = lax.axis_size("x")
    width = mine.shape[-1]
    vmem = pl.BlockSpec(memory_space=pltpu.VMEM)
    return pl.pallas_call(
        encode_kernel,
        out_shape=jax.ShapeDtypeStruct((cols * tokens, width), jnp.bfloat16),
        in_specs=[pl.BlockSpec(memory_space=pltpu.SMEM)] + [vmem] * 8,
        out_specs=vmem,
        scratch_shapes=[pltpu.VMEM((depth, width), jnp.bfloat16)],
        cost_estimate=pl.CostEstimate(
            flops=2 * cols * tokens * depth * width,
            transcendentals=0,
            bytes_accessed=2 * (cols * tokens * depth + depth * width + cols * tokens * width),
        ),
        name="encode",
    )(place, *parts, mine, other, bias)


def rows_of(weight, slot, block):
    per_core = weight.shape[2]
    quarter = weight[:, slot // per_core, slot % per_core, block]
    return quarter.reshape(-1, quarter.shape[-1])


def decode_kernel(layout, place, *refs):
    *parts, weight, bias, out = refs
    col, cols = place[0], weight.shape[3]
    upper = pl.program_id(0) < pl.num_programs(0) // 2
    summed, queue = bias[...], list(parts)
    for slot, step, halved in layout:
        part = queue.pop(0)[...]
        if halved:
            part = jnp.where(upper, part, queue.pop(0)[...])
        block = rows_of(weight, slot, at_step(col, cols, step))
        summed = summed + jnp.dot(part, block, preferred_element_type=jnp.float32)
    out[...] = summed


def last_kernel(place, top, bottom, weight, carried, out):
    upper = pl.program_id(0) < pl.num_programs(0) // 2
    part = jnp.where(upper, top[...], bottom[...])
    block = weight[...].reshape(part.shape[1], weight.shape[-1])
    summed = carried[...] + jnp.dot(part, block, preferred_element_type=jnp.float32)
    out[0, 0] = summed.astype(out.dtype)


def tiles(cols, tokens, quarter, half):
    mid = cols // 2
    pick = {
        None: lambda i, *_: (i, 0),
        "top": lambda i, *_: (jnp.minimum(i, mid - 1), 0),
        "bottom": lambda i, *_: (jnp.maximum(i - mid, 0), 0),
    }[half]
    return pl.BlockSpec((tokens, quarter), pick)


def decode(place, layout, parts, weight, bias):
    cols = lax.axis_size("x")
    rows, quarter = parts[0].shape
    tokens, width = rows // cols, weight.shape[-1]
    specs = []
    for _, _, halved in layout:
        for half in ("top", "bottom") if halved else (None,):
            specs.append(tiles(cols, tokens, quarter, half))
    return pl.pallas_call(
        functools.partial(decode_kernel, layout),
        out_shape=jax.ShapeDtypeStruct((rows, width), jnp.float32),
        grid_spec=pltpu.PrefetchScalarGridSpec(
            num_scalar_prefetch=1,
            grid=(cols,),
            in_specs=[
                *specs,
                pl.BlockSpec(weight.shape, lambda i, place: (0,) * weight.ndim),
                pl.BlockSpec(bias.shape, lambda i, place: (0, 0)),
            ],
            out_specs=pl.BlockSpec((tokens, width), lambda i, place: (i, 0)),
        ),
        cost_estimate=pl.CostEstimate(
            flops=2 * rows * quarter * len(layout) * width,
            transcendentals=0,
            bytes_accessed=2 * quarter * len(layout) * (rows + width) + 4 * rows * width,
        ),
        name="decode",
    )(place, *parts, weight, bias)


def decode_last(place, top, bottom, weight, slot, carried):
    cols = lax.axis_size("x")
    rows, width = carried.shape
    quarter = top.shape[1]
    tokens = rows // cols
    y_size, _, per_core, _, own, _ = weight.shape

    def across(i, place):
        return 0, slot // per_core, slot % per_core, at_step(place[0], cols, 3), 0, 0

    return pl.pallas_call(
        last_kernel,
        out_shape=jax.ShapeDtypeStruct((1, cols, tokens, width), jnp.bfloat16),
        grid_spec=pltpu.PrefetchScalarGridSpec(
            num_scalar_prefetch=1,
            grid=(cols,),
            in_specs=[
                tiles(cols, tokens, quarter, "top"),
                tiles(cols, tokens, quarter, "bottom"),
                pl.BlockSpec((y_size, 1, 1, 1, own, width), across),
                pl.BlockSpec((tokens, width), lambda i, place: (i, 0)),
            ],
            out_specs=pl.BlockSpec((1, 1, tokens, width), lambda i, place: (0, i, 0, 0)),
        ),
        cost_estimate=pl.CostEstimate(
            flops=2 * rows * quarter * width,
            transcendentals=0,
            bytes_accessed=2 * quarter * (rows + width) + 6 * rows * width,
        ),
        name="decode_last",
    )(place, top, bottom, weight, carried)


def forward(inputs, enc_weight, enc_bias, dec_weight, dec_bias):
    layers, _, latent_count = enc_weight.shape
    width = dec_weight.shape[2]
    layer, col, core = lax.axis_index("zl"), lax.axis_index("x"), lax.axis_index("core")
    cols = lax.axis_size("x")
    col_width = width // cols
    quarter = latent_count // cols
    place = jnp.stack([col, core]).astype(jnp.int32)

    near = exchange(inputs[0], False, 0)
    flip = exchange(inputs[0], True, 0)
    parts = (inputs[0], near, flip, *halves(near, flip, 0))

    own = lax.dynamic_slice(
        enc_weight, (layer, 0, col * quarter), (1, enc_weight.shape[1], quarter)
    )[0]
    over_zh = spread(own, "zh")
    mine = spread(over_zh, "y")
    other = lax.ppermute(mine, "core", [(0, 1), (1, 0)])

    blocks = []
    for slot in range(layers):
        pair = layer * (layer + 1) // 2 + jnp.maximum(layer - slot, 0)
        blocks.append(
            lax.dynamic_slice(
                dec_weight, (pair, 0, col * col_width), (1, dec_weight.shape[1], col_width)
            )
        )
    cores, zh_size, y_size = lax.axis_size("core"), lax.axis_size("zh"), lax.axis_size("y")
    over_z = lax.all_gather(jnp.concatenate(blocks, 0), ("zh", "core"), axis=1, tiled=False)
    per_core = layers // cores
    share = lax.dynamic_slice_in_dim(over_z, core * per_core, per_core, 0)
    decoder = lax.all_gather(share, ("y", "core"), axis=0, tiled=False)
    decoder = decoder.reshape(y_size, cores, per_core, zh_size, -1, col_width)

    bias = lax.dynamic_slice(enc_bias, (layer, col * quarter), (1, quarter))
    held = encode(place, parts, mine, other, bias)

    layout, blocks = [], []
    for slot in range(layers):
        following = None
        if slot < layers - 1:
            following = lax.ppermute(
                held, "zl", [(i, i + 1) for i in range(slot, layers - 1)]
            )
        near = exchange(held, False, slot)
        flip = exchange(held, True, slot)
        layout += [(slot, 0, False), (slot, 1, False), (slot, 2, False)]
        blocks += [held, near, flip]
        if slot in (0, layers - 1):
            far = halves(near, flip, slot)
        elif slot % 2:
            far = (exchange(flip, False, slot),)
        else:
            far = (exchange(near, True, slot),)
        if slot < layers - 1:
            layout.append((slot, 3, len(far) == 2))
            blocks += far
        held = following
    group_bias = lax.dynamic_slice(dec_bias, (layer, col * col_width), (1, col_width))
    carried = decode(place, tuple(layout), blocks, decoder, group_bias)
    return decode_last(place, *far, decoder, layers - 1, carried)


def solution(mesh):
    names = dict(zip(mesh.axis_names, mesh.devices.shape))
    layers, zh_size, cores = 4, 4, 2
    cols = names["layer"] // layers
    y_size = names["tok"] // (zh_size * cores)
    grid = Mesh(mesh.devices.reshape(layers, cols, zh_size, y_size, cores), AXES)
    in_specs = (P(LAYER, TOK, None), P(None, TOK, None), P(), P(None, TOK, None), P())
    out_specs = P(LAYER, None, TOK, None)
    return jax.shard_map(forward, mesh=grid, in_specs=in_specs, out_specs=out_specs, check_vma=False)
```

```python
import functools

import jax
import jax.numpy as jnp
from jax import lax
from jax.experimental import pallas as pl
from jax.experimental.pallas import tpu as pltpu
from jax.sharding import Mesh, PartitionSpec as P


AXES = ("zl", "x", "zh", "y", "core")
LAYER = ("zl", "x")
TOK = ("zh", "y", "core")


def spread(block, axis):
    size = lax.axis_size(axis)
    return lax.all_to_all(
        jnp.broadcast_to(block[None], (size, *block.shape)), axis, 0, 0, tiled=True
    )


def exchange(block, flip, least):
    cols, layers = lax.axis_size("x"), lax.axis_size("zl")
    pairs = [
        (layer * cols + i, layer * cols + (cols - 1 - i if flip else i ^ 1))
        for layer in range(least, layers)
        for i in range(cols)
    ]
    return lax.ppermute(block, LAYER, pairs)


def halves(near, flipped, least):
    mid = near.shape[0] // 2
    top = exchange(near[:mid], True, least)
    bottom = exchange(flipped[mid:], False, least)
    return top, bottom


def at_step(col, cols, step):
    near = col + 1 - 2 * lax.rem(col, 2)
    return (col, near, cols - 1 - col, lax.rem(col + 2, cols))[step]


def encode_kernel(place, own, near, flip, top, bottom, mine, other, bias, out, weight):
    col, core = place[0], place[1]
    y_size, zh_size, rows, _ = mine.shape
    cols = out.shape[0] // own.shape[0]
    for zh in range(zh_size):
        for y in range(y_size):
            start = (zh * y_size + y) * 2 * rows
            weight[pl.ds(pl.multiple_of(start + core * rows, rows), rows), :] = mine[y, zh]
            weight[pl.ds(pl.multiple_of(start + (1 - core) * rows, rows), rows), :] = other[y, zh]
    tokens, mid = own.shape[0], top.shape[0]
    for step, part, offset in ((0, own, 0), (1, near, 0), (2, flip, 0), (3, top, 0), (3, bottom, mid)):
        group = at_step(col, cols, step)
        preact = jnp.dot(part[...], weight[...], preferred_element_type=jnp.float32)
        latents = jnp.maximum(preact + bias[...], 0.0).astype(out.dtype)
        out[pl.ds(pl.multiple_of(group * tokens + offset, mid), part.shape[0]), :] = latents


def encode(place, parts, mine, other, bias):
    tokens, depth = parts[0].shape
    cols = lax.axis_size("x")
    width = mine.shape[-1]
    vmem = pl.BlockSpec(memory_space=pltpu.VMEM)
    return pl.pallas_call(
        encode_kernel,
        out_shape=jax.ShapeDtypeStruct((cols * tokens, width), jnp.bfloat16),
        in_specs=[pl.BlockSpec(memory_space=pltpu.SMEM)] + [vmem] * 8,
        out_specs=vmem,
        scratch_shapes=[pltpu.VMEM((depth, width), jnp.bfloat16)],
        cost_estimate=pl.CostEstimate(
            flops=2 * cols * tokens * depth * width,
            transcendentals=0,
            bytes_accessed=2 * (cols * tokens * depth + depth * width + cols * tokens * width),
        ),
        name="encode",
    )(place, *parts, mine, other, bias)


def rows_of(weight, slot, block):
    per_core = weight.shape[2]
    quarter = weight[:, slot // per_core, slot % per_core, block]
    return quarter.reshape(-1, quarter.shape[-1])


def decode_kernel(layout, place, *refs):
    *parts, weight, carried, out = refs
    col, cols = place[0], weight.shape[3]
    upper = pl.program_id(0) < pl.num_programs(0) // 2
    summed, queue = carried[...], list(parts)
    for slot, step, halved in layout:
        part = queue.pop(0)[...]
        if halved:
            part = jnp.where(upper, part, queue.pop(0)[...])
        block = rows_of(weight, slot, at_step(col, cols, step))
        summed = summed + jnp.dot(part, block, preferred_element_type=jnp.float32)
    out[...] = summed


def last_kernel(place, top, bottom, weight, carried, out):
    part = jnp.where(pl.program_id(0) == 0, top[...], bottom[...])
    block = weight[...].reshape(part.shape[1], weight.shape[-1])
    summed = carried[...] + jnp.dot(part, block, preferred_element_type=jnp.float32)
    out[0] = summed.astype(out.dtype).reshape(out.shape[1:])


def tiles(cols, tokens, quarter, half):
    mid = cols // 2
    pick = {
        None: lambda i, *_: (i, 0),
        "top": lambda i, *_: (jnp.minimum(i, mid - 1), 0),
        "bottom": lambda i, *_: (jnp.maximum(i - mid, 0), 0),
    }[half]
    return pl.BlockSpec((tokens, quarter), pick)


def decode(place, layout, parts, weight, carried):
    cols = lax.axis_size("x")
    rows, quarter = parts[0].shape
    tokens, width = rows // cols, weight.shape[-1]
    specs = []
    for _, _, halved in layout:
        for half in ("top", "bottom") if halved else (None,):
            specs.append(tiles(cols, tokens, quarter, half))
    return pl.pallas_call(
        functools.partial(decode_kernel, layout),
        out_shape=jax.ShapeDtypeStruct((rows, width), jnp.float32),
        grid_spec=pltpu.PrefetchScalarGridSpec(
            num_scalar_prefetch=1,
            grid=(cols,),
            in_specs=[
                *specs,
                pl.BlockSpec(weight.shape, lambda i, place: (0,) * weight.ndim),
                pl.BlockSpec(
                    (min(tokens, carried.shape[0]), width),
                    lambda i, place: (i if carried.shape[0] == rows else 0, 0),
                ),
            ],
            out_specs=pl.BlockSpec((tokens, width), lambda i, place: (i, 0)),
        ),
        cost_estimate=pl.CostEstimate(
            flops=2 * rows * quarter * len(layout) * width,
            transcendentals=0,
            bytes_accessed=2 * quarter * len(layout) * (rows + width) + 4 * rows * width,
        ),
        name="decode",
    )(place, *parts, weight, carried)


def decode_last(place, top, bottom, weight, slot, carried):
    cols = lax.axis_size("x")
    rows, width = carried.shape
    quarter = top.shape[1]
    tokens = rows // cols
    y_size, _, per_core, _, own, _ = weight.shape

    def across(i, place):
        return 0, slot // per_core, slot % per_core, at_step(place[0], cols, 3), 0, 0

    return pl.pallas_call(
        last_kernel,
        out_shape=jax.ShapeDtypeStruct((1, cols, tokens, width), jnp.bfloat16),
        grid_spec=pltpu.PrefetchScalarGridSpec(
            num_scalar_prefetch=1,
            grid=(2,),
            in_specs=[
                pl.BlockSpec(top.shape, lambda i, place: (0, 0)),
                pl.BlockSpec(bottom.shape, lambda i, place: (0, 0)),
                pl.BlockSpec((y_size, 1, 1, 1, own, width), across),
                pl.BlockSpec((rows // 2, width), lambda i, place: (i, 0)),
            ],
            out_specs=pl.BlockSpec((1, cols // 2, tokens, width), lambda i, place: (0, i, 0, 0)),
        ),
        cost_estimate=pl.CostEstimate(
            flops=2 * rows * quarter * width,
            transcendentals=0,
            bytes_accessed=2 * quarter * (rows + width) + 6 * rows * width,
        ),
        name="decode_last",
    )(place, top, bottom, weight, carried)


def forward(inputs, enc_weight, enc_bias, dec_weight, dec_bias):
    layers, _, latent_count = enc_weight.shape
    width = dec_weight.shape[2]
    layer, col, core = lax.axis_index("zl"), lax.axis_index("x"), lax.axis_index("core")
    cols = lax.axis_size("x")
    col_width = width // cols
    quarter = latent_count // cols
    place = jnp.stack([col, core]).astype(jnp.int32)

    near = exchange(inputs[0], False, 0)
    flip = exchange(inputs[0], True, 0)
    parts = (inputs[0], near, flip, *halves(near, flip, 0))

    own = lax.dynamic_slice(
        enc_weight, (layer, 0, col * quarter), (1, enc_weight.shape[1], quarter)
    )[0]
    over_zh = spread(own, "zh")
    mine = spread(over_zh, "y")
    other = lax.ppermute(mine, "core", [(0, 1), (1, 0)])

    blocks = []
    for slot in range(layers):
        pair = layer * (layer + 1) // 2 + jnp.maximum(layer - slot, 0)
        blocks.append(
            lax.dynamic_slice(
                dec_weight, (pair, 0, col * col_width), (1, dec_weight.shape[1], col_width)
            )
        )
    cores, zh_size, y_size = lax.axis_size("core"), lax.axis_size("zh"), lax.axis_size("y")
    over_z = lax.all_gather(jnp.concatenate(blocks, 0), ("zh", "core"), axis=1, tiled=False)
    per_core = layers // cores
    share = lax.dynamic_slice_in_dim(over_z, core * per_core, per_core, 0)
    decoder = lax.all_gather(share, ("y", "core"), axis=0, tiled=False)
    decoder = decoder.reshape(y_size, cores, per_core, zh_size, -1, col_width)

    bias = lax.dynamic_slice(enc_bias, (layer, col * quarter), (1, quarter))
    held = encode(place, parts, mine, other, bias)

    early, late = [], []
    for slot in range(layers):
        following = None
        if slot < layers - 1:
            following = lax.ppermute(
                held, "zl", [(i, i + 1) for i in range(slot, layers - 1)]
            )
        near = exchange(held, False, slot)
        flip = exchange(held, True, slot)
        stage = early if slot < layers - 1 else late
        stage += [((slot, step, False), (block,)) for step, block in enumerate((held, near, flip))]
        if slot in (0, layers - 1):
            far = halves(near, flip, slot)
        elif slot % 2:
            far = (exchange(flip, False, slot),)
        else:
            far = (exchange(near, True, slot),)
        if slot < layers - 1:
            stage = late if slot else early
            stage.append(((slot, 3, len(far) == 2), far))
        held = following
    carried = lax.dynamic_slice(dec_bias, (layer, col * col_width), (1, col_width))
    for stage in (early, late):
        layout = tuple(entry for entry, _ in stage)
        blocks = [block for _, group in stage for block in group]
        carried = decode(place, layout, blocks, decoder, carried)
    return decode_last(place, *far, decoder, layers - 1, carried)


def solution(mesh):
    names = dict(zip(mesh.axis_names, mesh.devices.shape))
    layers, zh_size, cores = 4, 4, 2
    cols = names["layer"] // layers
    y_size = names["tok"] // (zh_size * cores)
    grid = Mesh(mesh.devices.reshape(layers, cols, zh_size, y_size, cores), AXES)
    in_specs = (P(LAYER, TOK, None), P(None, TOK, None), P(), P(None, TOK, None), P())
    out_specs = P(LAYER, None, TOK, None)
    return jax.shard_map(forward, mesh=grid, in_specs=in_specs, out_specs=out_specs, check_vma=False)
```

```python
import functools

import jax
import jax.numpy as jnp
from jax import lax
from jax.experimental import pallas as pl
from jax.experimental.pallas import tpu as pltpu
from jax.sharding import Mesh, PartitionSpec as P


AXES = ("zl", "x", "zh", "y", "core")
LAYER = ("zl", "x")
TOK = ("zh", "y", "core")


def spread(block, axis):
    size = lax.axis_size(axis)
    return lax.all_to_all(
        jnp.broadcast_to(block[None], (size, *block.shape)), axis, 0, 0, tiled=True
    )


def exchange(block, flip, least):
    cols, layers = lax.axis_size("x"), lax.axis_size("zl")
    pairs = [
        (layer * cols + i, layer * cols + (cols - 1 - i if flip else i ^ 1))
        for layer in range(least, layers)
        for i in range(cols)
    ]
    return lax.ppermute(block, LAYER, pairs)


def halves(near, flipped, least):
    mid = near.shape[0] // 2
    top = exchange(near[:mid], True, least)
    bottom = exchange(flipped[mid:], False, least)
    return top, bottom


def in_vmem(array):
    return pltpu.with_memory_space_constraint(array, pltpu.VMEM)


def at_step(col, cols, step):
    near = col + 1 - 2 * lax.rem(col, 2)
    return (col, near, cols - 1 - col, lax.rem(col + 2, cols))[step]


def encode_kernel(place, own, near, flip, top, bottom, mine, other, bias, out, weight):
    col, core = place[0], place[1]
    y_size, zh_size, rows, _ = mine.shape
    cols = out.shape[0] // own.shape[0]
    for zh in range(zh_size):
        for y in range(y_size):
            start = (zh * y_size + y) * 2 * rows
            weight[pl.ds(pl.multiple_of(start + core * rows, rows), rows), :] = mine[y, zh]
            weight[pl.ds(pl.multiple_of(start + (1 - core) * rows, rows), rows), :] = other[y, zh]
    tokens, mid = own.shape[0], top.shape[0]
    for step, part, offset in ((0, own, 0), (1, near, 0), (2, flip, 0), (3, top, 0), (3, bottom, mid)):
        group = at_step(col, cols, step)
        preact = jnp.dot(part[...], weight[...], preferred_element_type=jnp.float32)
        latents = jnp.maximum(preact + bias[...], 0.0).astype(out.dtype)
        out[pl.ds(pl.multiple_of(group * tokens + offset, mid), part.shape[0]), :] = latents


def encode(place, parts, mine, other, bias):
    tokens, depth = parts[0].shape
    cols = lax.axis_size("x")
    width = mine.shape[-1]
    vmem = pl.BlockSpec(memory_space=pltpu.VMEM)
    return pl.pallas_call(
        encode_kernel,
        out_shape=jax.ShapeDtypeStruct((cols * tokens, width), jnp.bfloat16),
        in_specs=[pl.BlockSpec(memory_space=pltpu.SMEM)] + [vmem] * 8,
        out_specs=vmem,
        scratch_shapes=[pltpu.VMEM((depth, width), jnp.bfloat16)],
        cost_estimate=pl.CostEstimate(
            flops=2 * cols * tokens * depth * width,
            transcendentals=0,
            bytes_accessed=2 * (cols * tokens * depth + depth * width + cols * tokens * width),
        ),
        compiler_params=pltpu.CompilerParams(vmem_limit_bytes=16 << 20),
        name="encode",
    )(place, parts[0], *map(in_vmem, parts[1:]), mine, in_vmem(other), bias)


def rows_of(weight, slot, block):
    per_core = weight.shape[2]
    quarter = weight[:, slot // per_core, slot % per_core, block]
    return quarter.reshape(-1, quarter.shape[-1])


def decode_kernel(layout, place, *refs):
    *parts, weight, carried, out = refs
    col, cols = place[0], weight.shape[3]
    rows = cols * out.shape[2] if len(out.shape) == 4 else out.shape[0]
    tokens, mid = rows // cols, rows // 2
    for group in range(cols):
        at = group * tokens
        queue = list(parts)
        summed = carried[...] if carried.shape[0] == 1 else carried[pl.ds(at, tokens), :]
        for slot, step, halved in layout:
            part, start = queue.pop(0), at
            if halved:
                bottom = queue.pop(0)
                part, start = (part, at) if at < mid else (bottom, at - mid)
            block = rows_of(weight, slot, at_step(col, cols, step))
            piece = part[pl.ds(start, tokens), :]
            summed = summed + jnp.dot(piece, block, preferred_element_type=jnp.float32)
        if len(out.shape) == 2:
            out[pl.ds(at, tokens), :] = summed
        else:
            out[0, group] = summed.astype(out.dtype)


def decode(place, layout, parts, weight, carried, rows, last):
    cols = lax.axis_size("x")
    quarter, width = parts[0].shape[1], weight.shape[-1]
    if last:
        out_shape = jax.ShapeDtypeStruct((1, cols, rows // cols, width), jnp.bfloat16)
    else:
        out_shape = jax.ShapeDtypeStruct((rows, width), jnp.float32)
    vmem = pl.BlockSpec(memory_space=pltpu.VMEM)
    return pl.pallas_call(
        functools.partial(decode_kernel, layout),
        out_shape=out_shape,
        in_specs=[pl.BlockSpec(memory_space=pltpu.SMEM)] + [vmem] * (len(parts) + 2),
        out_specs=vmem,
        cost_estimate=pl.CostEstimate(
            flops=2 * rows * quarter * len(layout) * width,
            transcendentals=0,
            bytes_accessed=2 * quarter * len(layout) * (rows + width) + 4 * rows * width,
        ),
        compiler_params=pltpu.CompilerParams(vmem_limit_bytes=16 << 20),
        name="decode",
    )(place, *map(in_vmem, parts), weight, in_vmem(carried) if carried.shape[0] == rows else carried)


def forward(inputs, enc_weight, enc_bias, dec_weight, dec_bias):
    layers, _, latent_count = enc_weight.shape
    width = dec_weight.shape[2]
    layer, col, core = lax.axis_index("zl"), lax.axis_index("x"), lax.axis_index("core")
    cols = lax.axis_size("x")
    col_width = width // cols
    quarter = latent_count // cols
    place = jnp.stack([col, core]).astype(jnp.int32)

    near = exchange(inputs[0], False, 0)
    flip = exchange(inputs[0], True, 0)
    parts = (inputs[0], near, flip, *halves(near, flip, 0))

    own = lax.dynamic_slice(
        enc_weight, (layer, 0, col * quarter), (1, enc_weight.shape[1], quarter)
    )[0]
    over_zh = spread(own, "zh")
    mine = spread(over_zh, "y")
    other = lax.ppermute(mine, "core", [(0, 1), (1, 0)])

    blocks = []
    for slot in range(layers):
        pair = layer * (layer + 1) // 2 + jnp.maximum(layer - slot, 0)
        blocks.append(
            lax.dynamic_slice(
                dec_weight, (pair, 0, col * col_width), (1, dec_weight.shape[1], col_width)
            )
        )
    cores, zh_size, y_size = lax.axis_size("core"), lax.axis_size("zh"), lax.axis_size("y")
    over_z = lax.all_gather(jnp.concatenate(blocks, 0), ("zh", "core"), axis=1, tiled=False)
    per_core = layers // cores
    share = lax.dynamic_slice_in_dim(over_z, core * per_core, per_core, 0)
    decoder = lax.all_gather(share, ("y", "core"), axis=0, tiled=False)
    decoder = decoder.reshape(y_size, cores, per_core, zh_size, -1, col_width)

    bias = lax.dynamic_slice(enc_bias, (layer, col * quarter), (1, quarter))
    held = latents = encode(place, parts, mine, other, bias)

    early, late = [], []
    for slot in range(layers):
        following = None
        if slot < layers - 1:
            following = lax.ppermute(
                held, "zl", [(i, i + 1) for i in range(slot, layers - 1)]
            )
        near = exchange(held, False, slot)
        flip = exchange(held, True, slot)
        stage = early if slot < layers - 1 else late
        stage += [((slot, step, False), (block,)) for step, block in enumerate((held, near, flip))]
        if slot in (0, layers - 1):
            far = halves(near, flip, slot)
        elif slot % 2:
            far = (exchange(flip, False, slot),)
        else:
            far = (exchange(near, True, slot),)
        if slot < layers - 1:
            stage = late if slot else early
            stage.append(((slot, 3, len(far) == 2), far))
        held = following
    carried = lax.dynamic_slice(dec_bias, (layer, col * col_width), (1, col_width))
    decoder = in_vmem(decoder)
    final = [((layers - 1, 3, True), far)]
    for stage in (early, late, final):
        layout = tuple(entry for entry, _ in stage)
        blocks = [block for _, group in stage for block in group]
        carried = decode(place, layout, blocks, decoder, carried, latents.shape[0], stage is final)
    return carried


def solution(mesh):
    names = dict(zip(mesh.axis_names, mesh.devices.shape))
    layers, zh_size, cores = 4, 4, 2
    cols = names["layer"] // layers
    y_size = names["tok"] // (zh_size * cores)
    grid = Mesh(mesh.devices.reshape(layers, cols, zh_size, y_size, cores), AXES)
    in_specs = (P(LAYER, TOK, None), P(None, TOK, None), P(), P(None, TOK, None), P())
    out_specs = P(LAYER, None, TOK, None)
    return jax.shard_map(forward, mesh=grid, in_specs=in_specs, out_specs=out_specs, check_vma=False)
```

```python
import functools

import jax
import jax.numpy as jnp
from jax import lax
from jax.experimental import pallas as pl
from jax.experimental.pallas import tpu as pltpu
from jax.sharding import Mesh, PartitionSpec as P


AXES = ("zl", "x", "zh", "y", "core")
LAYER = ("zl", "x")
TOK = ("zh", "y", "core")


def spread(block, axis):
    size = lax.axis_size(axis)
    return lax.all_to_all(
        jnp.broadcast_to(block[None], (size, *block.shape)), axis, 0, 0, tiled=True
    )


def exchange(block, flip, least):
    cols, layers = lax.axis_size("x"), lax.axis_size("zl")
    pairs = [
        (layer * cols + i, layer * cols + (cols - 1 - i if flip else i ^ 1))
        for layer in range(least, layers)
        for i in range(cols)
    ]
    return lax.ppermute(block, LAYER, pairs)


def halves(near, flipped, least):
    mid = near.shape[0] // 2
    top = exchange(near[:mid], True, least)
    bottom = exchange(flipped[mid:], False, least)
    return top, bottom


def in_vmem(array):
    return pltpu.with_memory_space_constraint(array, pltpu.VMEM)


def in_hbm(array):
    return pltpu.with_memory_space_constraint(array, pltpu.HBM)


def at_step(col, cols, step):
    near = col + 1 - 2 * lax.rem(col, 2)
    return (col, near, cols - 1 - col, lax.rem(col + 2, cols))[step]


def encode_kernel(
    place, own_hbm, near, flip, top, bottom, mine_hbm, other, bias, out, weight, own, mine, sems
):
    col, core = place[0], place[1]
    fetch_mine = pltpu.make_async_copy(mine_hbm, mine, sems.at[0])
    fetch_own = pltpu.make_async_copy(own_hbm, own, sems.at[1])
    fetch_mine.start()
    fetch_own.start()
    fetch_mine.wait()
    y_size, zh_size, rows, _ = mine.shape
    cols = out.shape[0] // own.shape[0]
    for zh in range(zh_size):
        for y in range(y_size):
            start = (zh * y_size + y) * 2 * rows
            weight[pl.ds(pl.multiple_of(start + core * rows, rows), rows), :] = mine[y, zh]
            weight[pl.ds(pl.multiple_of(start + (1 - core) * rows, rows), rows), :] = other[y, zh]
    tokens, mid = own.shape[0], top.shape[0]
    for step, part, offset in ((1, near, 0), (2, flip, 0), (3, top, 0), (3, bottom, mid), (0, own, 0)):
        if step == 0:
            fetch_own.wait()
        group = at_step(col, cols, step)
        preact = jnp.dot(part[...], weight[...], preferred_element_type=jnp.float32)
        latents = jnp.maximum(preact + bias[...], 0.0).astype(out.dtype)
        out[pl.ds(pl.multiple_of(group * tokens + offset, mid), part.shape[0]), :] = latents


def encode(place, parts, mine, other, bias):
    tokens, depth = parts[0].shape
    cols = lax.axis_size("x")
    width = mine.shape[-1]
    vmem = pl.BlockSpec(memory_space=pltpu.VMEM)
    return pl.pallas_call(
        encode_kernel,
        out_shape=jax.ShapeDtypeStruct((cols * tokens, width), jnp.bfloat16),
        in_specs=[
            pl.BlockSpec(memory_space=pltpu.SMEM),
            pl.BlockSpec(memory_space=pltpu.HBM),
            *[vmem] * 4,
            pl.BlockSpec(memory_space=pltpu.HBM),
            *[vmem] * 2,
        ],
        out_specs=vmem,
        scratch_shapes=[
            pltpu.VMEM((depth, width), jnp.bfloat16),
            pltpu.VMEM((tokens, depth), jnp.bfloat16),
            pltpu.VMEM(mine.shape, jnp.bfloat16),
            pltpu.SemaphoreType.DMA((2,)),
        ],
        cost_estimate=pl.CostEstimate(
            flops=2 * cols * tokens * depth * width,
            transcendentals=0,
            bytes_accessed=2 * (cols * tokens * depth + depth * width + cols * tokens * width),
        ),
        compiler_params=pltpu.CompilerParams(vmem_limit_bytes=16 << 20),
        name="encode",
    )(place, in_hbm(parts[0]), *map(in_vmem, parts[1:]), in_hbm(mine), in_vmem(other), bias)


def rows_of(weight, slot, block):
    per_core = weight.shape[2]
    quarter = weight[:, slot // per_core, slot % per_core, block]
    return quarter.reshape(-1, quarter.shape[-1])


def decode_kernel(layout, place, *refs):
    *parts, weight, carried, out = refs
    col, cols = place[0], weight.shape[3]
    rows = cols * out.shape[2] if len(out.shape) == 4 else out.shape[0]
    tokens, mid = rows // cols, rows // 2
    for group in range(cols):
        at = group * tokens
        queue = list(parts)
        summed = carried[...] if carried.shape[0] == 1 else carried[pl.ds(at, tokens), :]
        for slot, step, halved in layout:
            part, start = queue.pop(0), at
            if halved:
                bottom = queue.pop(0)
                part, start = (part, at) if at < mid else (bottom, at - mid)
            block = rows_of(weight, slot, at_step(col, cols, step))
            piece = part[pl.ds(start, tokens), :]
            summed = summed + jnp.dot(piece, block, preferred_element_type=jnp.float32)
        if len(out.shape) == 2:
            out[pl.ds(at, tokens), :] = summed
        else:
            out[0, group] = summed.astype(out.dtype)


def decode(place, layout, parts, weight, carried, rows, last):
    cols = lax.axis_size("x")
    quarter, width = parts[0].shape[1], weight.shape[-1]
    if last:
        out_shape = jax.ShapeDtypeStruct((1, cols, rows // cols, width), jnp.bfloat16)
    else:
        out_shape = jax.ShapeDtypeStruct((rows, width), jnp.float32)
    vmem = pl.BlockSpec(memory_space=pltpu.VMEM)
    return pl.pallas_call(
        functools.partial(decode_kernel, layout),
        out_shape=out_shape,
        in_specs=[pl.BlockSpec(memory_space=pltpu.SMEM)] + [vmem] * (len(parts) + 2),
        out_specs=vmem,
        cost_estimate=pl.CostEstimate(
            flops=2 * rows * quarter * len(layout) * width,
            transcendentals=0,
            bytes_accessed=2 * quarter * len(layout) * (rows + width) + 4 * rows * width,
        ),
        compiler_params=pltpu.CompilerParams(vmem_limit_bytes=16 << 20),
        name="decode",
    )(place, *map(in_vmem, parts), weight, in_vmem(carried) if carried.shape[0] == rows else carried)


def forward(inputs, enc_weight, enc_bias, dec_weight, dec_bias):
    layers, _, latent_count = enc_weight.shape
    width = dec_weight.shape[2]
    layer, col, core = lax.axis_index("zl"), lax.axis_index("x"), lax.axis_index("core")
    cols = lax.axis_size("x")
    col_width = width // cols
    quarter = latent_count // cols
    place = jnp.stack([col, core]).astype(jnp.int32)

    near = exchange(inputs[0], False, 0)
    flip = exchange(inputs[0], True, 0)
    parts = (inputs[0], near, flip, *halves(near, flip, 0))

    own = lax.dynamic_slice(
        enc_weight, (layer, 0, col * quarter), (1, enc_weight.shape[1], quarter)
    )[0]
    over_zh = spread(own, "zh")
    mine = spread(over_zh, "y")
    other = lax.ppermute(mine, "core", [(0, 1), (1, 0)])

    blocks = []
    for slot in range(layers):
        pair = layer * (layer + 1) // 2 + jnp.maximum(layer - slot, 0)
        blocks.append(
            lax.dynamic_slice(
                dec_weight, (pair, 0, col * col_width), (1, dec_weight.shape[1], col_width)
            )
        )
    cores, zh_size, y_size = lax.axis_size("core"), lax.axis_size("zh"), lax.axis_size("y")
    over_z = lax.all_gather(jnp.concatenate(blocks, 0), ("zh", "core"), axis=1, tiled=False)
    per_core = layers // cores
    share = lax.dynamic_slice_in_dim(over_z, core * per_core, per_core, 0)
    decoder = lax.all_gather(share, ("y", "core"), axis=0, tiled=False)
    decoder = decoder.reshape(y_size, cores, per_core, zh_size, -1, col_width)

    bias = lax.dynamic_slice(enc_bias, (layer, col * quarter), (1, quarter))
    held = latents = encode(place, parts, mine, other, bias)

    early, late, final = [], [], []
    for slot in range(layers):
        following = None
        if slot < layers - 1:
            following = lax.ppermute(
                held, "zl", [(i, i + 1) for i in range(slot, layers - 1)]
            )
        near = exchange(held, False, slot)
        flip = exchange(held, True, slot)
        stage = early if slot < layers - 1 else late
        stage += [((slot, step, False), (block,)) for step, block in enumerate((held, near, flip))]
        if slot == 0:
            far = first_far = exchange(near, True, slot)
        elif slot == layers - 1:
            far = lax.ppermute(first_far, "zl", [(0, layers - 1)])
        elif slot == 1:
            far = exchange(near, True, slot)
        else:
            far = exchange(flip, False, slot)
        stage = {0: early, layers - 1: late}.get(slot, final)
        stage.append(((slot, 3, False), (far,)))
        held = following
    carried = lax.dynamic_slice(dec_bias, (layer, col * col_width), (1, col_width))
    decoder = in_vmem(decoder)
    for stage in (early, late, final):
        layout = tuple(entry for entry, _ in stage)
        blocks = [block for _, group in stage for block in group]
        carried = decode(place, layout, blocks, decoder, carried, latents.shape[0], stage is final)
    return carried


def solution(mesh):
    names = dict(zip(mesh.axis_names, mesh.devices.shape))
    layers, zh_size, cores = 4, 4, 2
    cols = names["layer"] // layers
    y_size = names["tok"] // (zh_size * cores)
    grid = Mesh(mesh.devices.reshape(layers, cols, zh_size, y_size, cores), AXES)
    in_specs = (P(LAYER, TOK, None), P(None, TOK, None), P(), P(None, TOK, None), P())
    out_specs = P(LAYER, None, TOK, None)
    return jax.shard_map(forward, mesh=grid, in_specs=in_specs, out_specs=out_specs, check_vma=False)
```

```python
import functools

import jax
import jax.numpy as jnp
from jax import lax
from jax.experimental import pallas as pl
from jax.experimental.pallas import tpu as pltpu
from jax.sharding import Mesh, PartitionSpec as P


AXES = ("zl", "x", "zh", "y", "core")
LAYER = ("zl", "x")
TOK = ("zh", "y", "core")


def spread(block, axis):
    size = lax.axis_size(axis)
    return lax.all_to_all(
        jnp.broadcast_to(block[None], (size, *block.shape)), axis, 0, 0, tiled=True
    )


def exchange(block, flip, least):
    cols, layers = lax.axis_size("x"), lax.axis_size("zl")
    pairs = [
        (layer * cols + i, layer * cols + (cols - 1 - i if flip else i ^ 1))
        for layer in range(least, layers)
        for i in range(cols)
    ]
    return lax.ppermute(block, LAYER, pairs)


def halves(near, flipped, least):
    mid = near.shape[0] // 2
    top = exchange(near[:mid], True, least)
    bottom = exchange(flipped[mid:], False, least)
    return top, bottom


def in_vmem(array):
    return pltpu.with_memory_space_constraint(array, pltpu.VMEM)


def at_step(col, cols, step):
    near = col + 1 - 2 * lax.rem(col, 2)
    return (col, near, cols - 1 - col, lax.rem(col + 2, cols))[step]


def encode_kernel(place, own, near, flip, top, bottom, mine, other, bias, out, weight):
    col, core = place[0], place[1]
    y_size, zh_size, rows, _ = mine.shape
    cols = out.shape[0] // own.shape[0]
    for zh in range(zh_size):
        for y in range(y_size):
            start = (zh * y_size + y) * 2 * rows
            weight[pl.ds(pl.multiple_of(start + core * rows, rows), rows), :] = mine[y, zh]
            weight[pl.ds(pl.multiple_of(start + (1 - core) * rows, rows), rows), :] = other[y, zh]
    tokens, mid = own.shape[0], top.shape[0]
    for step, part, offset in ((0, own, 0), (1, near, 0), (2, flip, 0), (3, top, 0), (3, bottom, mid)):
        group = at_step(col, cols, step)
        preact = jnp.dot(part[...], weight[...], preferred_element_type=jnp.float32)
        latents = jnp.maximum(preact + bias[...], 0.0).astype(out.dtype)
        out[pl.ds(pl.multiple_of(group * tokens + offset, mid), part.shape[0]), :] = latents


def encode(place, parts, mine, other, bias):
    tokens, depth = parts[0].shape
    cols = lax.axis_size("x")
    width = mine.shape[-1]
    vmem = pl.BlockSpec(memory_space=pltpu.VMEM)
    return pl.pallas_call(
        encode_kernel,
        out_shape=jax.ShapeDtypeStruct((cols * tokens, width), jnp.bfloat16),
        in_specs=[pl.BlockSpec(memory_space=pltpu.SMEM)] + [vmem] * 8,
        out_specs=vmem,
        scratch_shapes=[pltpu.VMEM((depth, width), jnp.bfloat16)],
        cost_estimate=pl.CostEstimate(
            flops=2 * cols * tokens * depth * width,
            transcendentals=0,
            bytes_accessed=2 * (cols * tokens * depth + depth * width + cols * tokens * width),
        ),
        compiler_params=pltpu.CompilerParams(vmem_limit_bytes=16 << 20),
        name="encode",
    )(place, parts[0], *map(in_vmem, parts[1:]), mine, in_vmem(other), bias)


def rows_of(weight, slot, block):
    per_core = weight.shape[2]
    quarter = weight[:, slot // per_core, slot % per_core, block]
    return quarter.reshape(-1, quarter.shape[-1])


def decode_kernel(layout, place, *refs):
    *parts, weight, carried, out = refs
    col, cols = place[0], weight.shape[3]
    rows = cols * out.shape[2] if len(out.shape) == 4 else out.shape[0]
    tokens, mid = rows // cols, rows // 2
    for group in range(cols):
        at = group * tokens
        queue = list(parts)
        summed = carried[...] if carried.shape[0] == 1 else carried[pl.ds(at, tokens), :]
        for slot, step, halved in layout:
            part, start = queue.pop(0), at
            if halved:
                bottom = queue.pop(0)
                part, start = (part, at) if at < mid else (bottom, at - mid)
            block = rows_of(weight, slot, at_step(col, cols, step))
            piece = part[pl.ds(start, tokens), :]
            summed = summed + jnp.dot(piece, block, preferred_element_type=jnp.float32)
        if len(out.shape) == 2:
            out[pl.ds(at, tokens), :] = summed
        else:
            out[0, group] = summed.astype(out.dtype)


def decode(place, layout, parts, weight, carried, rows, last):
    cols = lax.axis_size("x")
    quarter, width = parts[0].shape[1], weight.shape[-1]
    if last:
        out_shape = jax.ShapeDtypeStruct((1, cols, rows // cols, width), jnp.bfloat16)
    else:
        out_shape = jax.ShapeDtypeStruct((rows, width), jnp.float32)
    vmem = pl.BlockSpec(memory_space=pltpu.VMEM)
    return pl.pallas_call(
        functools.partial(decode_kernel, layout),
        out_shape=out_shape,
        in_specs=[pl.BlockSpec(memory_space=pltpu.SMEM)] + [vmem] * (len(parts) + 2),
        out_specs=vmem,
        cost_estimate=pl.CostEstimate(
            flops=2 * rows * quarter * len(layout) * width,
            transcendentals=0,
            bytes_accessed=2 * quarter * len(layout) * (rows + width) + 4 * rows * width,
        ),
        compiler_params=pltpu.CompilerParams(vmem_limit_bytes=16 << 20),
        name="decode",
    )(place, *map(in_vmem, parts), weight, in_vmem(carried) if carried.shape[0] == rows else carried)


def forward(inputs, enc_weight, enc_bias, dec_weight, dec_bias):
    layers, _, latent_count = enc_weight.shape
    width = dec_weight.shape[2]
    layer, col, core = lax.axis_index("zl"), lax.axis_index("x"), lax.axis_index("core")
    cols = lax.axis_size("x")
    col_width = width // cols
    quarter = latent_count // cols
    place = jnp.stack([col, core]).astype(jnp.int32)

    near = exchange(inputs[0], False, 0)
    flip = exchange(inputs[0], True, 0)
    parts = (inputs[0], near, flip, *halves(near, flip, 0))

    own = lax.dynamic_slice(
        enc_weight, (layer, 0, col * quarter), (1, enc_weight.shape[1], quarter)
    )[0]
    over_zh = spread(own, "zh")
    mine = spread(over_zh, "y")
    other = lax.ppermute(mine, "core", [(0, 1), (1, 0)])

    blocks = []
    for slot in range(layers):
        pair = layer * (layer + 1) // 2 + jnp.maximum(layer - slot, 0)
        blocks.append(
            lax.dynamic_slice(
                dec_weight, (pair, 0, col * col_width), (1, dec_weight.shape[1], col_width)
            )
        )
    cores, zh_size, y_size = lax.axis_size("core"), lax.axis_size("zh"), lax.axis_size("y")
    over_z = lax.all_gather(jnp.concatenate(blocks, 0), ("zh", "core"), axis=1, tiled=False)
    per_core = layers // cores
    share = lax.dynamic_slice_in_dim(over_z, core * per_core, per_core, 0)
    decoder = lax.all_gather(share, ("y", "core"), axis=0, tiled=False)
    decoder = decoder.reshape(y_size, cores, per_core, zh_size, -1, col_width)

    bias = lax.dynamic_slice(enc_bias, (layer, col * quarter), (1, quarter))
    held = latents = encode(place, parts, mine, other, bias)

    early, late, final = [], [], []
    for slot in range(layers):
        following = None
        if slot < layers - 1:
            following = lax.ppermute(
                held, "zl", [(i, i + 1) for i in range(slot, layers - 1)]
            )
        near = exchange(held, False, slot)
        flip = exchange(held, True, slot)
        stage = early if slot < layers - 1 else late
        stage += [((slot, step, False), (block,)) for step, block in enumerate((held, near, flip))]
        if slot == 0:
            far = jnp.concatenate(halves(near, flip, slot), 0)
            relayed = lax.ppermute(far, "zl", [(0, layers - 2)])
        elif slot == layers - 1:
            far = lax.ppermute(relayed, "zl", [(layers - 2, layers - 1)])
        elif slot == 1:
            far = exchange(near, True, slot)
        else:
            far = exchange(flip, False, slot)
        stage = {0: early, layers - 1: late}.get(slot, final)
        stage.append(((slot, 3, False), (far,)))
        held = following
    carried = lax.dynamic_slice(dec_bias, (layer, col * col_width), (1, col_width))
    decoder = in_vmem(decoder)
    for stage in (early, late, final):
        layout = tuple(entry for entry, _ in stage)
        blocks = [block for _, group in stage for block in group]
        carried = decode(place, layout, blocks, decoder, carried, latents.shape[0], stage is final)
    return carried


def solution(mesh):
    names = dict(zip(mesh.axis_names, mesh.devices.shape))
    layers, zh_size, cores = 4, 4, 2
    cols = names["layer"] // layers
    y_size = names["tok"] // (zh_size * cores)
    grid = Mesh(mesh.devices.reshape(layers, cols, zh_size, y_size, cores), AXES)
    in_specs = (P(LAYER, TOK, None), P(None, TOK, None), P(), P(None, TOK, None), P())
    out_specs = P(LAYER, None, TOK, None)
    return jax.shard_map(forward, mesh=grid, in_specs=in_specs, out_specs=out_specs, check_vma=False)
```

```python
import functools

import jax
import jax.numpy as jnp
from jax import lax
from jax.experimental import pallas as pl
from jax.experimental.pallas import tpu as pltpu
from jax.sharding import Mesh, PartitionSpec as P


AXES = ("zl", "x", "zh", "y", "core")
LAYER = ("zl", "x")
TOK = ("zh", "y", "core")


def spread(block, axis):
    size = lax.axis_size(axis)
    return lax.all_to_all(
        jnp.broadcast_to(block[None], (size, *block.shape)), axis, 0, 0, tiled=True
    )


def exchange(block, flip, least):
    cols, layers = lax.axis_size("x"), lax.axis_size("zl")
    pairs = [
        (layer * cols + i, layer * cols + (cols - 1 - i if flip else i ^ 1))
        for layer in range(least, layers)
        for i in range(cols)
    ]
    return lax.ppermute(block, LAYER, pairs)


def halves(near, flipped, least):
    mid = near.shape[0] // 2
    top = exchange(near[:mid], True, least)
    bottom = exchange(flipped[mid:], False, least)
    return top, bottom


def in_vmem(array):
    return pltpu.with_memory_space_constraint(array, pltpu.VMEM)


def at_step(col, cols, step):
    near = col + 1 - 2 * lax.rem(col, 2)
    return (col, near, cols - 1 - col, lax.rem(col + 2, cols))[step]


def encode_kernel(place, own, near, flip, top, bottom, mine, other, bias, out, weight):
    col, core = place[0], place[1]
    y_size, zh_size, rows, _ = mine.shape
    cols = out.shape[0] // own.shape[0]
    for zh in range(zh_size):
        for y in range(y_size):
            start = (zh * y_size + y) * 2 * rows
            weight[pl.ds(pl.multiple_of(start + core * rows, rows), rows), :] = mine[y, zh]
            weight[pl.ds(pl.multiple_of(start + (1 - core) * rows, rows), rows), :] = other[y, zh]
    tokens, mid = own.shape[0], top.shape[0]
    for step, part, offset in ((0, own, 0), (1, near, 0), (2, flip, 0), (3, top, 0), (3, bottom, mid)):
        group = at_step(col, cols, step)
        preact = jnp.dot(part[...], weight[...], preferred_element_type=jnp.float32)
        latents = jnp.maximum(preact + bias[...], 0.0).astype(out.dtype)
        out[pl.ds(pl.multiple_of(group * tokens + offset, mid), part.shape[0]), :] = latents


def encode(place, parts, mine, other, bias):
    tokens, depth = parts[0].shape
    cols = lax.axis_size("x")
    width = mine.shape[-1]
    vmem = pl.BlockSpec(memory_space=pltpu.VMEM)
    return pl.pallas_call(
        encode_kernel,
        out_shape=jax.ShapeDtypeStruct((cols * tokens, width), jnp.bfloat16),
        in_specs=[pl.BlockSpec(memory_space=pltpu.SMEM)] + [vmem] * 8,
        out_specs=vmem,
        scratch_shapes=[pltpu.VMEM((depth, width), jnp.bfloat16)],
        cost_estimate=pl.CostEstimate(
            flops=2 * cols * tokens * depth * width,
            transcendentals=0,
            bytes_accessed=2 * (cols * tokens * depth + depth * width + cols * tokens * width),
        ),
        compiler_params=pltpu.CompilerParams(vmem_limit_bytes=16 << 20),
        name="encode",
    )(place, parts[0], *map(in_vmem, parts[1:]), mine, in_vmem(other), bias)


def rows_of(weight, slot, block):
    per_core = weight.shape[2]
    quarter = weight[:, slot // per_core, slot % per_core, block]
    return quarter.reshape(-1, quarter.shape[-1])


def decode_kernel(layout, place, *refs):
    *parts, weight, carried, out = refs
    col, cols = place[0], weight.shape[3]
    rows = cols * out.shape[2] if len(out.shape) == 4 else out.shape[0]
    tokens, mid = rows // cols, rows // 2
    least = min(slot for slot, _, _ in layout)

    def products(filled):
        for group in range(cols):
            at = group * tokens
            queue = list(parts)
            summed = carried[...] if carried.shape[0] == 1 else carried[pl.ds(at, tokens), :]
            for slot, step, halved in layout if filled else ():
                part, start = queue.pop(0), at
                if halved:
                    bottom = queue.pop(0)
                    part, start = (part, at) if at < mid else (bottom, at - mid)
                block = rows_of(weight, slot, at_step(col, cols, step))
                piece = part[pl.ds(start, tokens), :]
                summed = summed + jnp.dot(piece, block, preferred_element_type=jnp.float32)
            if len(out.shape) == 2:
                out[pl.ds(at, tokens), :] = summed
            else:
                out[0, group] = summed.astype(out.dtype)

    if least:
        pl.when(place[2] >= least)(lambda: products(True))
        pl.when(place[2] < least)(lambda: products(False))
    else:
        products(True)


def decode(place, layout, parts, weight, carried, rows, last):
    cols = lax.axis_size("x")
    quarter, width = parts[0].shape[1], weight.shape[-1]
    if last:
        out_shape = jax.ShapeDtypeStruct((1, cols, rows // cols, width), jnp.bfloat16)
    else:
        out_shape = jax.ShapeDtypeStruct((rows, width), jnp.float32)
    vmem = pl.BlockSpec(memory_space=pltpu.VMEM)
    return pl.pallas_call(
        functools.partial(decode_kernel, layout),
        out_shape=out_shape,
        in_specs=[pl.BlockSpec(memory_space=pltpu.SMEM)] + [vmem] * (len(parts) + 2),
        out_specs=vmem,
        cost_estimate=pl.CostEstimate(
            flops=2 * rows * quarter * len(layout) * width,
            transcendentals=0,
            bytes_accessed=2 * quarter * len(layout) * (rows + width) + 4 * rows * width,
        ),
        compiler_params=pltpu.CompilerParams(vmem_limit_bytes=16 << 20),
        name="decode",
    )(place, *map(in_vmem, parts), weight, in_vmem(carried) if carried.shape[0] == rows else carried)


def forward(inputs, enc_weight, enc_bias, dec_weight, dec_bias):
    layers, _, latent_count = enc_weight.shape
    width = dec_weight.shape[2]
    layer, col, core = lax.axis_index("zl"), lax.axis_index("x"), lax.axis_index("core")
    cols = lax.axis_size("x")
    col_width = width // cols
    quarter = latent_count // cols
    place = jnp.stack([col, core, layer]).astype(jnp.int32)

    near = exchange(inputs[0], False, 0)
    flip = exchange(inputs[0], True, 0)
    parts = (inputs[0], near, flip, *halves(near, flip, 0))

    own = lax.dynamic_slice(
        enc_weight, (layer, 0, col * quarter), (1, enc_weight.shape[1], quarter)
    )[0]
    over_zh = spread(own, "zh")
    mine = spread(over_zh, "y")
    other = lax.ppermute(mine, "core", [(0, 1), (1, 0)])

    blocks = []
    for slot in range(layers):
        pair = layer * (layer + 1) // 2 + jnp.maximum(layer - slot, 0)
        blocks.append(
            lax.dynamic_slice(
                dec_weight, (pair, 0, col * col_width), (1, dec_weight.shape[1], col_width)
            )
        )
    cores, zh_size, y_size = lax.axis_size("core"), lax.axis_size("zh"), lax.axis_size("y")
    over_z = lax.all_gather(jnp.concatenate(blocks, 0), ("zh", "core"), axis=1, tiled=False)
    per_core = layers // cores
    share = lax.dynamic_slice_in_dim(over_z, core * per_core, per_core, 0)
    decoder = lax.all_gather(share, ("y", "core"), axis=0, tiled=False)
    decoder = decoder.reshape(y_size, cores, per_core, zh_size, -1, col_width)

    bias = lax.dynamic_slice(enc_bias, (layer, col * quarter), (1, quarter))
    held = latents = encode(place, parts, mine, other, bias)

    early, late, final = [], [], []
    for slot in range(layers):
        following = None
        if slot < layers - 1:
            following = lax.ppermute(
                held, "zl", [(i, i + 1) for i in range(slot, layers - 1)]
            )
        near = exchange(held, False, slot)
        flip = exchange(held, True, slot)
        for step, block in enumerate((held, near, flip)):
            stage = early if slot < layers - 1 else final if step else late
            stage.append(((slot, step, False), (block,)))
        if slot == 0:
            far = jnp.concatenate(halves(near, flip, slot), 0)
            relayed = lax.ppermute(far, "zl", [(i, i + 2) for i in range(layers - 2)])
        elif slot == layers - 1:
            far = lax.ppermute(relayed, "zl", [(layers - 2, layers - 1)])
        elif slot == 1:
            far = halves(near, flip, slot)
        else:
            far = relayed
        stage = (early, late, late, final)[slot]
        far = far if slot == 1 else (far,)
        stage.append(((slot, 3, slot == 1), far))
        held = following
    carried = lax.dynamic_slice(dec_bias, (layer, col * col_width), (1, col_width))
    decoder = in_vmem(decoder)
    for stage in (early, late, final):
        layout = tuple(entry for entry, _ in stage)
        blocks = [block for _, group in stage for block in group]
        carried = decode(place, layout, blocks, decoder, carried, latents.shape[0], stage is final)
    return carried


def solution(mesh):
    names = dict(zip(mesh.axis_names, mesh.devices.shape))
    layers, zh_size, cores = 4, 4, 2
    cols = names["layer"] // layers
    y_size = names["tok"] // (zh_size * cores)
    grid = Mesh(mesh.devices.reshape(layers, cols, zh_size, y_size, cores), AXES)
    in_specs = (P(LAYER, TOK, None), P(None, TOK, None), P(), P(None, TOK, None), P())
    out_specs = P(LAYER, None, TOK, None)
    return jax.shard_map(forward, mesh=grid, in_specs=in_specs, out_specs=out_specs, check_vma=False)
```

```python
import functools

import jax
import jax.numpy as jnp
from jax import lax
from jax.experimental import pallas as pl
from jax.experimental.pallas import tpu as pltpu
from jax.sharding import Mesh, PartitionSpec as P


AXES = ("zl", "x", "zh", "y", "core")
LAYER = ("zl", "x")
TOK = ("zh", "y", "core")


def spread(block, axis):
    size = lax.axis_size(axis)
    return lax.all_to_all(
        jnp.broadcast_to(block[None], (size, *block.shape)), axis, 0, 0, tiled=True
    )


def exchange(block, flip, least):
    cols, layers = lax.axis_size("x"), lax.axis_size("zl")
    pairs = [
        (layer * cols + i, layer * cols + (cols - 1 - i if flip else i ^ 1))
        for layer in range(least, layers)
        for i in range(cols)
    ]
    return lax.ppermute(block, LAYER, pairs)


def halves(near, flipped, least):
    mid = near.shape[0] // 2
    top = exchange(near[:mid], True, least)
    bottom = exchange(flipped[mid:], False, least)
    return top, bottom


def in_vmem(array):
    return pltpu.with_memory_space_constraint(array, pltpu.VMEM)


def at_step(col, cols, step):
    near = col + 1 - 2 * lax.rem(col, 2)
    return (col, near, cols - 1 - col, lax.rem(col + 2, cols))[step]


def encode_kernel(place, own, near, flip, top, bottom, mine, other, bias, out, weight):
    col, core = place[0], place[1]
    y_size, zh_size, rows, _ = mine.shape
    cols = out.shape[0] // own.shape[0]
    for zh in range(zh_size):
        for y in range(y_size):
            start = (zh * y_size + y) * 2 * rows
            weight[pl.ds(pl.multiple_of(start + core * rows, rows), rows), :] = mine[y, zh]
            weight[pl.ds(pl.multiple_of(start + (1 - core) * rows, rows), rows), :] = other[y, zh]
    tokens, mid = own.shape[0], top.shape[0]
    for step, part, offset in ((0, own, 0), (1, near, 0), (2, flip, 0), (3, top, 0), (3, bottom, mid)):
        group = at_step(col, cols, step)
        preact = jnp.dot(part[...], weight[...], preferred_element_type=jnp.float32)
        latents = jnp.maximum(preact + bias[...], 0.0).astype(out.dtype)
        out[pl.ds(pl.multiple_of(group * tokens + offset, mid), part.shape[0]), :] = latents


def encode(place, parts, mine, other, bias):
    tokens, depth = parts[0].shape
    cols = lax.axis_size("x")
    width = mine.shape[-1]
    vmem = pl.BlockSpec(memory_space=pltpu.VMEM)
    return pl.pallas_call(
        encode_kernel,
        out_shape=jax.ShapeDtypeStruct((cols * tokens, width), jnp.bfloat16),
        in_specs=[pl.BlockSpec(memory_space=pltpu.SMEM)] + [vmem] * 8,
        out_specs=vmem,
        scratch_shapes=[pltpu.VMEM((depth, width), jnp.bfloat16)],
        cost_estimate=pl.CostEstimate(
            flops=2 * cols * tokens * depth * width,
            transcendentals=0,
            bytes_accessed=2 * (cols * tokens * depth + depth * width + cols * tokens * width),
        ),
        compiler_params=pltpu.CompilerParams(vmem_limit_bytes=16 << 20),
        name="encode",
    )(place, parts[0], *map(in_vmem, parts[1:]), mine, in_vmem(other), bias)


def rows_of(weight, slot, block):
    per_core = weight.shape[2]
    quarter = weight[:, slot // per_core, slot % per_core, block]
    return quarter.reshape(-1, quarter.shape[-1])


def decode_kernel(layout, fetched, place, *refs):
    if fetched:
        *parts, weight, carried, out, rows_held, sems = refs
    else:
        *parts, weight, carried, out = refs
    col, cols = place[0], weight.shape[3]
    per_core, copies = weight.shape[2], []
    for index, (slot, step, _) in enumerate(layout if fetched else ()):
        source = weight.at[:, slot // per_core, slot % per_core, at_step(col, cols, step)]
        copies.append(pltpu.make_async_copy(source, rows_held.at[index], sems.at[index]))
        copies[-1].start()
    rows = cols * out.shape[2] if len(out.shape) == 4 else out.shape[0]
    tokens, mid = rows // cols, rows // 2
    least = min(slot for slot, _, _ in layout)

    def products(filled):
        for group in range(cols):
            at = group * tokens
            queue = list(parts)
            summed = carried[...] if carried.shape[0] == 1 else carried[pl.ds(at, tokens), :]
            for index, (slot, step, halved) in enumerate(layout if filled else ()):
                part, start = queue.pop(0), at
                if halved:
                    bottom = queue.pop(0)
                    part, start = (part, at) if at < mid else (bottom, at - mid)
                if fetched:
                    if group == 0:
                        copies[index].wait()
                    block = rows_held[index].reshape(-1, weight.shape[-1])
                else:
                    block = rows_of(weight, slot, at_step(col, cols, step))
                piece = part[pl.ds(start, tokens), :]
                summed = summed + jnp.dot(piece, block, preferred_element_type=jnp.float32)
            if len(out.shape) == 2:
                out[pl.ds(at, tokens), :] = summed
            else:
                out[0, group] = summed.astype(out.dtype)

    if least:
        pl.when(place[2] >= least)(lambda: products(True))
        pl.when(place[2] < least)(lambda: products(False))
    else:
        products(True)


def decode(place, layout, parts, weight, weight_space, carried, rows, last):
    cols = lax.axis_size("x")
    quarter, width = parts[0].shape[1], weight.shape[-1]
    if last:
        out_shape = jax.ShapeDtypeStruct((1, cols, rows // cols, width), jnp.bfloat16)
    else:
        out_shape = jax.ShapeDtypeStruct((rows, width), jnp.float32)
    fetched = weight_space == pltpu.HBM
    vmem = pl.BlockSpec(memory_space=pltpu.VMEM)
    held = (len(layout), weight.shape[0], *weight.shape[4:])
    scratch = [pltpu.VMEM(held, weight.dtype), pltpu.SemaphoreType.DMA((len(layout),))]
    return pl.pallas_call(
        functools.partial(decode_kernel, layout, fetched),
        out_shape=out_shape,
        in_specs=[
            pl.BlockSpec(memory_space=pltpu.SMEM),
            *[vmem] * len(parts),
            pl.BlockSpec(memory_space=weight_space),
            vmem,
        ],
        scratch_shapes=scratch if fetched else [],
        out_specs=vmem,
        cost_estimate=pl.CostEstimate(
            flops=2 * rows * quarter * len(layout) * width,
            transcendentals=0,
            bytes_accessed=2 * quarter * len(layout) * (rows + width) + 4 * rows * width,
        ),
        compiler_params=pltpu.CompilerParams(vmem_limit_bytes=16 << 20),
        name="decode",
    )(
        place,
        *map(in_vmem, parts),
        pltpu.with_memory_space_constraint(weight, weight_space),
        in_vmem(carried) if carried.shape[0] == rows else carried,
    )


def forward(inputs, enc_weight, enc_bias, dec_weight, dec_bias):
    layers, _, latent_count = enc_weight.shape
    width = dec_weight.shape[2]
    layer, col, core = lax.axis_index("zl"), lax.axis_index("x"), lax.axis_index("core")
    cols = lax.axis_size("x")
    col_width = width // cols
    quarter = latent_count // cols
    place = jnp.stack([col, core, layer]).astype(jnp.int32)

    near = exchange(inputs[0], False, 0)
    flip = exchange(inputs[0], True, 0)
    parts = (inputs[0], near, flip, *halves(near, flip, 0))

    own = lax.dynamic_slice(
        enc_weight, (layer, 0, col * quarter), (1, enc_weight.shape[1], quarter)
    )[0]
    over_zh = spread(own, "zh")
    mine = spread(over_zh, "y")
    other = lax.ppermute(mine, "core", [(0, 1), (1, 0)])

    blocks = []
    for slot in range(layers):
        pair = layer * (layer + 1) // 2 + jnp.maximum(layer - slot, 0)
        blocks.append(
            lax.dynamic_slice(
                dec_weight, (pair, 0, col * col_width), (1, dec_weight.shape[1], col_width)
            )
        )
    cores, zh_size, y_size = lax.axis_size("core"), lax.axis_size("zh"), lax.axis_size("y")
    over_z = lax.all_gather(jnp.concatenate(blocks, 0), ("zh", "core"), axis=1, tiled=False)
    per_core = layers // cores
    share = lax.dynamic_slice_in_dim(over_z, core * per_core, per_core, 0)
    decoder = lax.all_gather(share, ("y", "core"), axis=0, tiled=False)
    decoder = decoder.reshape(y_size, cores, per_core, zh_size, -1, col_width)

    bias = lax.dynamic_slice(enc_bias, (layer, col * quarter), (1, quarter))
    held = latents = encode(place, parts, mine, other, bias)

    early, late, final = [], [], []
    for slot in range(layers):
        following = None
        if slot < layers - 1:
            following = lax.ppermute(
                held, "zl", [(i, i + 1) for i in range(slot, layers - 1)]
            )
        near = exchange(held, False, slot)
        flip = exchange(held, True, slot)
        for step, block in enumerate((held, near, flip)):
            stage = (early, early, late, final if step else late)[slot]
            stage.append(((slot, step, False), (block,)))
        if slot == 0:
            far = jnp.concatenate(halves(near, flip, slot), 0)
            relayed = lax.ppermute(far, "zl", [(0, 2)])
            passed = lax.ppermute(far, "zl", [(1, 3)])
        elif slot == layers - 1:
            far = lax.ppermute(relayed, "zl", [(layers - 2, layers - 1)])
        elif slot == 1:
            far = halves(near, flip, slot)
        else:
            far = relayed
        stage = (early, late, late, final)[slot]
        far = far if slot == 1 else (far,)
        stage.append(((slot, 3, slot == 1), far))
        if slot == 2:
            stage.append(((slot, 3, False), (passed,)))
        held = following
    carried = lax.dynamic_slice(dec_bias, (layer, col * col_width), (1, col_width))
    for stage in (early, late, final):
        layout = tuple(entry for entry, _ in stage)
        blocks = [block for _, group in stage for block in group]
        space = pltpu.HBM if stage is early else pltpu.VMEM
        rows = latents.shape[0]
        carried = decode(
            place, layout, blocks, decoder, space, carried, rows, stage is final
        )
    return carried


def solution(mesh):
    names = dict(zip(mesh.axis_names, mesh.devices.shape))
    layers, zh_size, cores = 4, 4, 2
    cols = names["layer"] // layers
    y_size = names["tok"] // (zh_size * cores)
    grid = Mesh(mesh.devices.reshape(layers, cols, zh_size, y_size, cores), AXES)
    in_specs = (P(LAYER, TOK, None), P(None, TOK, None), P(), P(None, TOK, None), P())
    out_specs = P(LAYER, None, TOK, None)
    return jax.shard_map(forward, mesh=grid, in_specs=in_specs, out_specs=out_specs, check_vma=False)
```

```python
import functools

import jax
import jax.numpy as jnp
from jax import lax
from jax.experimental import pallas as pl
from jax.experimental.pallas import tpu as pltpu
from jax.sharding import Mesh, PartitionSpec as P


AXES = ("zl", "x", "zh", "y", "core")
LAYER = ("zl", "x")
TOK = ("zh", "y", "core")


def spread(block, axis):
    size = lax.axis_size(axis)
    return lax.all_to_all(
        jnp.broadcast_to(block[None], (size, *block.shape)), axis, 0, 0, tiled=True
    )


def exchange(block, flip, least):
    cols, layers = lax.axis_size("x"), lax.axis_size("zl")
    pairs = [
        (layer * cols + i, layer * cols + (cols - 1 - i if flip else i ^ 1))
        for layer in range(least, layers)
        for i in range(cols)
    ]
    return lax.ppermute(block, LAYER, pairs)


def halves(near, flipped, least):
    mid = near.shape[0] // 2
    top = exchange(near[:mid], True, least)
    bottom = exchange(flipped[mid:], False, least)
    return top, bottom


def in_vmem(array):
    return pltpu.with_memory_space_constraint(array, pltpu.VMEM)


def at_step(col, cols, step):
    near = col + 1 - 2 * lax.rem(col, 2)
    return (col, near, cols - 1 - col, lax.rem(col + 2, cols))[step]


def encode_kernel(place, own, near, flip, top, bottom, mine, other, bias, out, weight):
    col, core = place[0], place[1]
    y_size, zh_size, rows, _ = mine.shape
    cols = out.shape[0] // own.shape[0]
    for zh in range(zh_size):
        for y in range(y_size):
            start = (zh * y_size + y) * 2 * rows
            weight[pl.ds(pl.multiple_of(start + core * rows, rows), rows), :] = mine[y, zh]
            weight[pl.ds(pl.multiple_of(start + (1 - core) * rows, rows), rows), :] = other[y, zh]
    tokens, mid = own.shape[0], top.shape[0]
    for step, part, offset in ((0, own, 0), (1, near, 0), (2, flip, 0), (3, top, 0), (3, bottom, mid)):
        group = at_step(col, cols, step)
        preact = jnp.dot(part[...], weight[...], preferred_element_type=jnp.float32)
        latents = jnp.maximum(preact + bias[...], 0.0).astype(out.dtype)
        out[pl.ds(pl.multiple_of(group * tokens + offset, mid), part.shape[0]), :] = latents


def encode(place, parts, mine, other, bias):
    tokens, depth = parts[0].shape
    cols = lax.axis_size("x")
    width = mine.shape[-1]
    vmem = pl.BlockSpec(memory_space=pltpu.VMEM)
    return pl.pallas_call(
        encode_kernel,
        out_shape=jax.ShapeDtypeStruct((cols * tokens, width), jnp.bfloat16),
        in_specs=[pl.BlockSpec(memory_space=pltpu.SMEM)] + [vmem] * 8,
        out_specs=vmem,
        scratch_shapes=[pltpu.VMEM((depth, width), jnp.bfloat16)],
        cost_estimate=pl.CostEstimate(
            flops=2 * cols * tokens * depth * width,
            transcendentals=0,
            bytes_accessed=2 * (cols * tokens * depth + depth * width + cols * tokens * width),
        ),
        compiler_params=pltpu.CompilerParams(vmem_limit_bytes=16 << 20),
        name="encode",
    )(place, parts[0], *map(in_vmem, parts[1:]), mine, in_vmem(other), bias)


def rows_of(weight, slot, block):
    per_core = weight.shape[2]
    quarter = weight[:, slot // per_core, slot % per_core, block]
    return quarter.reshape(-1, quarter.shape[-1])


def decode_kernel(layout, fetched, place, *refs):
    if fetched:
        *parts, weight, carried, out, rows_held, sems = refs
    else:
        *parts, weight, carried, out = refs
    col, cols = place[0], weight.shape[3]
    per_core, copies = weight.shape[2], []
    for index, (slot, step, _) in enumerate(layout if fetched else ()):
        source = weight.at[:, slot // per_core, slot % per_core, at_step(col, cols, step)]
        copies.append(pltpu.make_async_copy(source, rows_held.at[index], sems.at[index]))
        copies[-1].start()
    rows = cols * out.shape[2] if len(out.shape) == 4 else out.shape[0]
    tokens, mid = rows // cols, rows // 2
    least = min(slot for slot, _, _ in layout)

    def products(filled):
        for group in range(cols):
            at = group * tokens
            queue = list(parts)
            summed = carried[...] if carried.shape[0] == 1 else carried[pl.ds(at, tokens), :]
            for index, (slot, step, halved) in enumerate(layout if filled else ()):
                part, start = queue.pop(0), at
                if halved:
                    bottom = queue.pop(0)
                    part, start = (part, at) if at < mid else (bottom, at - mid)
                if fetched:
                    if group == 0:
                        copies[index].wait()
                    block = rows_held[index].reshape(-1, weight.shape[-1])
                else:
                    block = rows_of(weight, slot, at_step(col, cols, step))
                piece = part[pl.ds(start, tokens), :]
                summed = summed + jnp.dot(piece, block, preferred_element_type=jnp.float32)
            if len(out.shape) == 2:
                out[pl.ds(at, tokens), :] = summed
            else:
                out[0, group] = summed.astype(out.dtype)

    if least:
        pl.when(place[2] >= least)(lambda: products(True))
        pl.when(place[2] < least)(lambda: products(False))
    else:
        products(True)


def decode(place, layout, parts, weight, weight_space, carried, rows, last):
    cols = lax.axis_size("x")
    quarter, width = parts[0].shape[1], weight.shape[-1]
    if last:
        out_shape = jax.ShapeDtypeStruct((1, cols, rows // cols, width), jnp.bfloat16)
    else:
        out_shape = jax.ShapeDtypeStruct((rows, width), jnp.float32)
    fetched = weight_space == pltpu.HBM
    vmem = pl.BlockSpec(memory_space=pltpu.VMEM)
    held = (len(layout), weight.shape[0], *weight.shape[4:])
    scratch = [pltpu.VMEM(held, weight.dtype), pltpu.SemaphoreType.DMA((len(layout),))]
    return pl.pallas_call(
        functools.partial(decode_kernel, layout, fetched),
        out_shape=out_shape,
        in_specs=[
            pl.BlockSpec(memory_space=pltpu.SMEM),
            *[vmem] * len(parts),
            pl.BlockSpec(memory_space=weight_space),
            vmem,
        ],
        scratch_shapes=scratch if fetched else [],
        out_specs=vmem,
        cost_estimate=pl.CostEstimate(
            flops=2 * rows * quarter * len(layout) * width,
            transcendentals=0,
            bytes_accessed=2 * quarter * len(layout) * (rows + width) + 4 * rows * width,
        ),
        compiler_params=pltpu.CompilerParams(vmem_limit_bytes=16 << 20),
        name="decode",
    )(
        place,
        *map(in_vmem, parts),
        pltpu.with_memory_space_constraint(weight, weight_space),
        in_vmem(carried) if carried.shape[0] == rows else carried,
    )


def forward(inputs, enc_weight, enc_bias, dec_weight, dec_bias):
    layers, _, latent_count = enc_weight.shape
    width = dec_weight.shape[2]
    layer, col, core = lax.axis_index("zl"), lax.axis_index("x"), lax.axis_index("core")
    cols = lax.axis_size("x")
    col_width = width // cols
    quarter = latent_count // cols
    place = jnp.stack([col, core, layer]).astype(jnp.int32)

    near = exchange(inputs[0], False, 0)
    flip = exchange(inputs[0], True, 0)
    parts = (inputs[0], near, flip, *halves(near, flip, 0))

    own = lax.dynamic_slice(
        enc_weight, (layer, 0, col * quarter), (1, enc_weight.shape[1], quarter)
    )[0]
    over_zh = spread(own, "zh")
    mine = spread(over_zh, "y")
    other = lax.ppermute(mine, "core", [(0, 1), (1, 0)])

    blocks = []
    for slot in range(layers):
        pair = layer * (layer + 1) // 2 + jnp.maximum(layer - slot, 0)
        blocks.append(
            lax.dynamic_slice(
                dec_weight, (pair, 0, col * col_width), (1, dec_weight.shape[1], col_width)
            )
        )
    cores, zh_size, y_size = lax.axis_size("core"), lax.axis_size("zh"), lax.axis_size("y")
    over_z = lax.all_gather(jnp.concatenate(blocks, 0), ("zh", "core"), axis=1, tiled=False)
    per_core = layers // cores
    share = lax.dynamic_slice_in_dim(over_z, core * per_core, per_core, 0)
    decoder = lax.all_gather(share, ("y", "core"), axis=0, tiled=False)
    decoder = decoder.reshape(y_size, cores, per_core, zh_size, -1, col_width)

    bias = lax.dynamic_slice(enc_bias, (layer, col * quarter), (1, quarter))
    held = latents = encode(place, parts, mine, other, bias)

    early, late, close, final = [], [], [], []
    for slot in range(layers):
        following = None
        if slot < layers - 1:
            following = lax.ppermute(
                held, "zl", [(i, i + 1) for i in range(slot, layers - 1)]
            )
        near = exchange(held, False, slot)
        flip = exchange(held, True, slot)
        for step, block in enumerate((held, near, flip)):
            stage = (early, early, late, close if step else late)[slot]
            stage.append(((slot, step, False), (block,)))
        if slot == 0:
            far = jnp.concatenate(halves(near, flip, slot), 0)
            relayed = lax.ppermute(far, "zl", [(0, 2)])
            passed = lax.ppermute(far, "zl", [(1, 3)])
        elif slot == layers - 1:
            far = lax.ppermute(relayed, "zl", [(layers - 2, layers - 1)])
        elif slot == 1:
            far = halves(near, flip, slot)
        else:
            far = relayed
        stage = (early, late, late, final)[slot]
        far = far if slot == 1 else (far,)
        stage.append(((slot, 3, slot == 1), far))
        if slot == 2:
            stage.append(((slot, 3, False), (passed,)))
        held = following
    carried = lax.dynamic_slice(dec_bias, (layer, col * col_width), (1, col_width))
    for stage in (early, late, close, final):
        layout = tuple(entry for entry, _ in stage)
        blocks = [block for _, group in stage for block in group]
        space = pltpu.HBM if stage is early else pltpu.VMEM
        rows = latents.shape[0]
        carried = decode(
            place, layout, blocks, decoder, space, carried, rows, stage is final
        )
    return carried


def solution(mesh):
    names = dict(zip(mesh.axis_names, mesh.devices.shape))
    layers, zh_size, cores = 4, 4, 2
    cols = names["layer"] // layers
    y_size = names["tok"] // (zh_size * cores)
    grid = Mesh(mesh.devices.reshape(layers, cols, zh_size, y_size, cores), AXES)
    in_specs = (P(LAYER, TOK, None), P(None, TOK, None), P(), P(None, TOK, None), P())
    out_specs = P(LAYER, None, TOK, None)
    return jax.shard_map(forward, mesh=grid, in_specs=in_specs, out_specs=out_specs, check_vma=False)
```
